512 devices in a mesh: wide: 64 (over z, x), narrow: 8 (over y, core).
Axes of the slice: x: 4, y: 4, z: 16, core: 2. Of those that a mesh axis runs over, the one named last changes fastest.
Arguments:
- integrals: bfloat16 [16384, 65536], P('wide', 'narrow'), may hold values from -0.0625 to 0.0625
- amp_tiles: bfloat16 [8, 786432], P('narrow', 'wide'), may hold values from -6 to 6
- row_orbitals: int32 [16384, 2], P('wide'), may hold values from 0 to 511
- orb_irrep: int32 [512], replicated, may hold values from 0 to 3
- occ_pairs: int32 [96, 2], replicated, may hold values from 0 to 15
- occ_irrep: int32 [16], replicated, may hold values from 0 to 3
Outputs:
- residual: float32 [16384, 96], P(('wide', 'narrow'))
The draws below stay inside these ranges and needn't reach their ends.
All inputs are finite; a program needn't handle non-finite values.
Results may differ from the reference program's by a relative error of at most 0.0003.
Values may be sent and summed in bfloat16 or wider, within the bound.
A program may use at most 64 MiB of HBM per device.

```python
import jax
import jax.numpy as jnp

NV = 512
NIRREP = 4
NOCC = 16
NPAIR = 96
COLS = 65536
ROWS = 16384
COL_DEV = 8192
N_NARROW = 8


def place_ends(result, stream_key, least, top_value):
    place = [jax.random.randint(jax.random.fold_in(stream_key, axis), (), 0, length) for axis, length in enumerate(result.shape)]
    longest = result.shape.index(max(result.shape))
    next_to = place[:longest] + [(place[longest] + 1) % result.shape[longest]] + place[longest + 1:]
    return result.at[tuple(place)].set(least).at[tuple(next_to)].set(top_value)


def strengthened(array, own_key, source, target, shards_of, factor):
    owner, partner = [(jnp.arange(array.shape[axis_at]) // (array.shape[axis_at] // shards_of)).reshape([-1 if axis == axis_at else 1 for axis in range(array.ndim)]) for axis_at in (source, target)]
    chosen = jax.random.permutation(own_key, shards_of)[partner]
    strong = (owner == chosen) | (owner == (partner + shards_of // 2) % shards_of)
    return jnp.where(strong, factor * array, array)


def shard_levels(key, extent, cuts, smallest, largest):
    def one(axis_at, shards_of):
        heights = jax.random.uniform(jax.random.fold_in(jax.random.fold_in(key, 6), axis_at), (shards_of,), jnp.float32, smallest / len(cuts), largest / len(cuts))
        return jnp.repeat(jnp.exp(heights), extent[axis_at] // shards_of).reshape((-1,) + (1,) * (len(extent) - axis_at - 1))

    level = one(*cuts[0])
    for cut in cuts[1:]:
        level = level * one(*cut)
    return level


def centred(key, extent, deviation, limit, pieces=(), held_as=jnp.bfloat16):
    values = deviation * jax.random.normal(key, extent, jnp.float32)
    if pieces:
        values = values * shard_levels(key, extent, pieces, -0.22, 0.18)
    return jnp.clip(values, -limit, limit).astype(held_as)


def bell_draw_with(own_key, shape, scale, reach, pieces, heavy, dtype=jnp.bfloat16):
    drawn = scale * jax.random.normal(own_key, shape, jnp.float32)
    if pieces:
        drawn = drawn * shard_levels(own_key, shape, pieces, -0.22, 0.18)
    return jnp.clip(strengthened(drawn, jax.random.fold_in(own_key, 3), *heavy), -reach, reach).astype(dtype)


def setup_inputs(seed: int = 0) -> dict:
    streams_of = jax.random.split(jax.random.key(seed), 7)
    return {
        "integrals": bell_draw_with(streams_of[0], (ROWS, COLS), COLS ** -0.5, 0.0625, ((0, 64), (1, 8)), (1, 0, 64, 4.0)),
        "amp_tiles": centred(streams_of[1], (N_NARROW, COL_DEV * NPAIR), 1.0, 6.0, ((0, 8), (1, 64))),
        "row_orbitals": place_ends(jax.random.randint(streams_of[2], (ROWS, 2), 0, NV), jax.random.fold_in(streams_of[2], 1), 0, NV - 1).astype(jnp.int32),
        "orb_irrep": place_ends(jax.random.randint(streams_of[3], (NV,), 0, NIRREP), jax.random.fold_in(streams_of[3], 1), 0, NIRREP - 1).astype(jnp.int32),
        "occ_pairs": place_ends(jax.random.randint(streams_of[4], (NPAIR, 2), 0, NOCC), jax.random.fold_in(streams_of[4], 1), 0, NOCC - 1).astype(jnp.int32),
        "occ_irrep": place_ends(jax.random.randint(streams_of[5], (NOCC,), 0, NIRREP), jax.random.fold_in(streams_of[5], 1), 0, NIRREP - 1).astype(jnp.int32),
    }


def reference(integrals, amp_tiles, row_orbitals, orb_irrep, occ_pairs, occ_irrep):
    amplitudes = amp_tiles.reshape(COLS, NPAIR)
    ladder = jnp.dot(integrals, amplitudes, preferred_element_type=jnp.float32)
    row_sym = jnp.bitwise_xor(orb_irrep[row_orbitals[:, 0]], orb_irrep[row_orbitals[:, 1]])
    pair_sym = jnp.bitwise_xor(occ_irrep[occ_pairs[:, 0]], occ_irrep[occ_pairs[:, 1]])
    keep = row_sym[:, None] == pair_sym[None, :]
    return jnp.where(keep, ladder, jnp.zeros_like(ladder))
```

```python
import functools

import jax
import jax.numpy as jnp
from jax import lax
from jax.experimental import pallas as pl
from jax.experimental.pallas import tpu as pltpu
from jax.sharding import PartitionSpec as P

MESH = pl.DeviceIdType.MESH
NX = 4
LANES = 128


def pair_lookup(orbitals, table):
    count, entries = orbitals.shape[1], table.shape[1]
    column = jnp.sum(
        jnp.where(
            lax.broadcasted_iota(jnp.int32, (entries, entries), 0)
            == lax.broadcasted_iota(jnp.int32, (entries, entries), 1),
            jnp.broadcast_to(table, (entries, entries)),
            0,
        ),
        axis=1,
        keepdims=True,
    )
    place = lax.broadcasted_iota(jnp.int32, (entries, count), 0)
    labels = [
        jnp.sum(jnp.where(place == orbitals[i : i + 1, :], column, 0), axis=0, keepdims=True) for i in range(2)
    ]
    return labels[0] ^ labels[1]


def kernel(
    amp_ref, integrals_ref, row_sym_ref, pair_sym_ref, out_ref,
    rows, upright, gathered, block, acc, parts, load_sem, arrive, sent, part_sent, part_arrive,
):
    n_wide, n_narrow = lax.axis_size("wide"), lax.axis_size("narrow")
    nz = n_wide // NX
    half = nz // 2
    pairs = gathered.shape[1]
    own_rows = out_ref.shape[0]
    wide, narrow = lax.axis_index("wide"), lax.axis_index("narrow")
    z, x = wide // NX, wide % NX

    def at(dz, dx):
        return ((z + dz + nz) % nz) * NX + (x + dx + NX) % NX

    load = pltpu.make_async_copy(integrals_ref, block, load_sem)
    load.start()

    barrier = pltpu.get_barrier_semaphore()
    for other in (at(1, 0), at(-1, 0), at(0, 1), at(0, -1)):
        pl.semaphore_signal(barrier, inc=1, device_id={"wide": other}, device_id_type=MESH)
    for step in range(1, n_narrow):
        pl.semaphore_signal(
            barrier, inc=1, device_id={"narrow": (narrow + step) % n_narrow}, device_id_type=MESH
        )

    period = 4 * pairs
    groups = amp_ref.shape[1] // period
    for g in range(groups):
        rows[g : g + 1, :] = amp_ref[0:1, g * period : (g + 1) * period].astype(jnp.float32)
    upright[...] = jnp.zeros_like(upright)
    for j in range(4):
        upright[pl.ds(j, groups, stride=4), 0:pairs] = rows[:, j * pairs : (j + 1) * pairs]
    gathered[wide] = upright[...].T[:pairs, :].astype(jnp.bfloat16)
    acc[...] = jnp.zeros_like(acc)

    pl.semaphore_wait(barrier, 4 + n_narrow - 1)

    def send(source, dz, dx):
        pltpu.make_async_remote_copy(
            src_ref=gathered.at[source],
            dst_ref=gathered.at[source],
            send_sem=sent,
            recv_sem=arrive.at[source],
            device_id={"wide": at(dz, dx)},
            device_id_type=MESH,
        ).start()

    def wait(source):
        pltpu.make_async_remote_copy(
            src_ref=gathered.at[source],
            dst_ref=gathered.at[source],
            send_sem=sent,
            recv_sem=arrive.at[source],
            device_id={"wide": at(1, 0)},
            device_id_type=MESH,
        ).wait_recv()

    def multiply(dz):
        wait(at(dz, 1))
        wait(at(dz, -2))
        base = ((z + dz + nz) % nz) * NX
        columns = pl.ds(pl.multiple_of(base * LANES, NX * LANES), NX * LANES)
        amplitudes = jnp.concatenate([gathered[base + i] for i in range(NX)], axis=1)
        acc[:, 0:pairs] += lax.dot_general(
            block[:, columns], amplitudes, (((1,), (1,)), ((), ())), preferred_element_type=jnp.float32
        )

    send(wide, 0, 1)
    send(wide, 1, 0)
    send(wide, -1, 0)
    send(wide, 0, -1)
    beside = at(0, -1)
    wait(beside)
    send(beside, 1, 0)
    send(beside, -1, 0)
    send(beside, 0, 1)
    load.wait()

    def step(d, carry):
        for sign, dx, outer, last in ((-1, 0, -1, half), (1, -1, 1, half), (1, 0, -1, half - 1), (-1, -1, 1, half - 1)):
            source = at(sign * d, dx)
            wait(source)
            if last == half:
                send(source, -sign, 0)
            else:
                @pl.when(d < last)
                def _():
                    send(source, -sign, 0)
            send(source, 0, outer)
        multiply(-(d - 1))

        @pl.when(d > 1)
        def _():
            multiply(d - 1)

        return carry

    lax.fori_loop(1, half, step, 0)
    for sign, dx, outer in ((-1, 0, -1), (1, -1, 1)):
        source = at(sign * half, dx)
        wait(source)
        send(source, 0, outer)
    multiply(-(half - 1))
    multiply(half - 1)
    multiply(-half)

    def part(step):
        to = (narrow + step) % n_narrow
        return pltpu.make_async_remote_copy(
            src_ref=acc.at[pl.ds(pl.multiple_of(to * own_rows, own_rows), own_rows)],
            dst_ref=parts.at[n_narrow - step],
            send_sem=part_sent.at[step],
            recv_sem=part_arrive.at[n_narrow - step],
            device_id={"narrow": to},
            device_id_type=MESH,
        )

    copies = [part(step) for step in range(1, n_narrow)]
    for copy in copies:
        copy.start()
    total = acc[pl.ds(pl.multiple_of(narrow * own_rows, own_rows), own_rows), :]
    for step, copy in zip(range(1, n_narrow), copies):
        pltpu.make_async_remote_copy(
            src_ref=parts.at[step],
            dst_ref=parts.at[step],
            send_sem=part_sent.at[step],
            recv_sem=part_arrive.at[step],
            device_id={"narrow": (narrow + step) % n_narrow},
            device_id_type=MESH,
        ).wait_recv()
        total += parts[step]
    keep = row_sym_ref[...] == pair_sym_ref[...]
    out_ref[...] = jnp.where(keep, total[:, 0:pairs], 0.0)
    for copy in copies:
        copy.wait_send()
    pltpu.make_async_remote_copy(
        src_ref=gathered.at[pl.ds(0, n_wide - 1)],
        dst_ref=gathered.at[pl.ds(0, n_wide - 1)],
        send_sem=sent,
        recv_sem=arrive.at[0],
        device_id={"wide": at(1, 0)},
        device_id_type=MESH,
    ).wait_send()


def lookup_irrep(orbitals, table):
    hits = orbitals[..., None] == jnp.arange(table.shape[0], dtype=jnp.int32)
    return jnp.sum(jnp.where(hits, table, 0), axis=-1)


def shards(n_wide, n_narrow, integrals, amp_tiles, row_orbitals, orb_irrep, occ_pairs, occ_irrep):
    pairs = occ_pairs.shape[0]
    n_rows, n_columns = integrals.shape
    own_rows = n_rows // n_narrow
    mine = lax.dynamic_slice_in_dim(row_orbitals, lax.axis_index("narrow") * own_rows, own_rows, 0)
    row_labels = lookup_irrep(mine, orb_irrep)
    pair_labels = lookup_irrep(occ_pairs, occ_irrep)
    row_sym = (row_labels[:, 0] ^ row_labels[:, 1])[:, None]
    pair_sym = (pair_labels[:, 0] ^ pair_labels[:, 1])[None, :]
    vmem = pl.BlockSpec(memory_space=pltpu.VMEM)
    anywhere = pl.BlockSpec(memory_space=pl.ANY)
    return pl.pallas_call(
        kernel,
        out_shape=jax.ShapeDtypeStruct((own_rows, pairs), jnp.float32),
        in_specs=[vmem, anywhere, vmem, vmem],
        out_specs=vmem,
        scratch_shapes=[
            pltpu.VMEM((LANES // 4, 4 * pairs), jnp.float32),
            pltpu.VMEM((LANES, LANES), jnp.float32),
            pltpu.VMEM((n_wide, pairs, LANES), jnp.bfloat16),
            pltpu.VMEM((n_rows, n_columns), jnp.bfloat16),
            pltpu.VMEM((n_rows, LANES), jnp.float32),
            pltpu.VMEM((n_narrow, own_rows, LANES), jnp.float32),
            pltpu.SemaphoreType.DMA,
            pltpu.SemaphoreType.DMA((n_wide,)),
            pltpu.SemaphoreType.DMA,
            pltpu.SemaphoreType.DMA((n_narrow,)),
            pltpu.SemaphoreType.DMA((n_narrow,)),
        ],
        compiler_params=pltpu.CompilerParams(
            collective_id=0, has_side_effects=True, vmem_limit_bytes=48 << 20
        ),
    )(amp_tiles, integrals, row_sym, pair_sym)


def solution(mesh):
    in_specs = (P("wide", "narrow"), P("narrow", "wide"), P("wide", None), P(), P(), P())
    out_specs = P(("wide", "narrow"), None)
    return jax.shard_map(
        functools.partial(shards, mesh.shape["wide"], mesh.shape["narrow"]),
        mesh=mesh, in_specs=in_specs, out_specs=out_specs, check_vma=False,
    )
```

```python
import functools

import jax
import jax.numpy as jnp
from jax import lax
from jax.experimental import pallas as pl
from jax.experimental.pallas import tpu as pltpu
from jax.sharding import PartitionSpec as P

MESH = pl.DeviceIdType.MESH
NX = 4
LANES = 128


def pair_symmetry(orbitals, table):
    count, entries = orbitals.shape[1], table.shape[1]
    diagonal = lax.broadcasted_iota(jnp.int32, (entries, entries), 0) == lax.broadcasted_iota(
        jnp.int32, (entries, entries), 1
    )
    column = jnp.sum(jnp.where(diagonal, table, 0), axis=1, keepdims=True)
    place = lax.broadcasted_iota(jnp.int32, (entries, count), 0)
    first, second = (
        jnp.sum(jnp.where(place == orbitals[i : i + 1, :], column, 0), axis=0, keepdims=True) for i in range(2)
    )
    return first ^ second


def kernel(
    integrals_ref, amp_ref, row_orbitals_ref, orb_ref, pairs_ref, occ_ref, out_ref,
    tile, row_orbitals, orb, occ_pairs, occ, row_sym, rows, upright, gathered, block, acc, parts,
    load_sem, small_sem, arrive, sent, part_sent, part_arrive,
):
    n_wide, n_narrow = lax.axis_size("wide"), lax.axis_size("narrow")
    nz = n_wide // NX
    half = nz // 2
    pairs = gathered.shape[1]
    own_rows = out_ref.shape[0]
    wide, narrow = lax.axis_index("wide"), lax.axis_index("narrow")
    z, x = wide // NX, wide % NX

    def at(dz, dx):
        return ((z + dz + nz) % nz) * NX + (x + dx + NX) % NX

    targets = [(sign * d, dx) for dx in (0, 1) for d in (1, 2) for sign in (1, -1)] + [(0, 1), (0, -1)]
    barrier = pltpu.get_barrier_semaphore()
    for dz, dx in targets:
        pl.semaphore_signal(barrier, inc=1, device_id={"wide": at(-dz, -dx)}, device_id_type=MESH)
    for step in range(1, n_narrow):
        pl.semaphore_signal(
            barrier, inc=1, device_id={"narrow": (narrow + step) % n_narrow}, device_id_type=MESH
        )

    small = [
        pltpu.make_async_copy(source, target, small_sem.at[i])
        for i, (source, target) in enumerate(
            (
                (amp_ref, tile), (row_orbitals_ref, row_orbitals), (orb_ref, orb), (pairs_ref, occ_pairs),
                (occ_ref, occ),
            )
        )
    ]
    for copy in small:
        copy.start()
    load = pltpu.make_async_copy(integrals_ref, block, load_sem)
    load.start()

    upright[...] = jnp.zeros_like(upright)
    acc[...] = jnp.zeros_like(acc)
    small[0].wait()
    period = 4 * pairs
    groups = tile.shape[1] // period
    for g in range(groups):
        rows[g : g + 1, :] = tile[0:1, g * period : (g + 1) * period].astype(jnp.float32)
    for j in range(4):
        upright[pl.ds(j, groups, stride=4), 0:pairs] = rows[:, j * pairs : (j + 1) * pairs]
    gathered[wide] = upright[...].T[:pairs, :].astype(jnp.bfloat16)

    pl.semaphore_wait(barrier, len(targets) + n_narrow - 1)

    def copy_of(source, dz, dx):
        return pltpu.make_async_remote_copy(
            src_ref=gathered.at[source],
            dst_ref=gathered.at[source],
            send_sem=sent,
            recv_sem=arrive.at[source],
            device_id={"wide": at(dz, dx)},
            device_id_type=MESH,
        )

    def send(source, dz, dx):
        copy_of(source, dz, dx).start()

    def wait(source):
        copy_of(source, 1, 0).wait_recv()

    def multiply(dz):
        wait(at(dz, 1))
        wait(at(dz, -2))
        base = ((z + dz + nz) % nz) * NX
        columns = pl.ds(pl.multiple_of(base * LANES, NX * LANES), NX * LANES)
        amplitudes = jnp.concatenate([gathered[base + i] for i in range(NX)], axis=1)
        acc[:, 0:pairs] += lax.dot_general(
            block[:, columns], amplitudes, (((1,), (1,)), ((), ())), preferred_element_type=jnp.float32
        )

    last = half // 2 - 1
    forward = ((1, 0, True), (-1, 1, True), (-1, 0, False), (1, 1, False))
    for sign, dx, far in forward:
        if far or last > 0:
            send(wide, 2 * sign, dx)
    for sign, dx, _ in forward:
        send(wide, sign, dx)
    send(wide, 0, 1)
    send(wide, 0, -1)

    for copy in small[1:]:
        copy.wait()
    symmetry = pair_symmetry(row_orbitals[...], orb[...])
    n_rows = symmetry.shape[1]
    diagonal = lax.broadcasted_iota(jnp.int32, (n_rows, n_rows), 0) == lax.broadcasted_iota(
        jnp.int32, (n_rows, n_rows), 1
    )
    row_sym[...] = jnp.broadcast_to(
        jnp.sum(jnp.where(diagonal, symmetry, 0), axis=1, keepdims=True), row_sym.shape
    )
    own_sym = row_sym[pl.ds(pl.multiple_of(narrow * own_rows, own_rows), own_rows), 0:pairs]
    keep = own_sym == pair_symmetry(occ_pairs[...], occ[...])

    beside = at(0, -1)
    wait(beside)
    send(beside, 0, 1)
    load.wait()

    for k in range(1, last + 1):
        for sign, dx, far in forward:
            source = at(-2 * k * sign, -dx)
            wait(source)
            if far or k < last:
                send(source, 2 * sign, 0)
            send(source, sign, 0)
            send(source, 0, 1 if dx else -1)
        for sign, dx, _ in forward:
            source = at(-(2 * k - 1) * sign, -dx)
            wait(source)
            send(source, 0, 1 if dx else -1)
        if k == 1:
            multiply(0)
        else:
            for d in (2 * k - 3, 2 * k - 2):
                multiply(d)
                multiply(-d)
    for sign, dx, far in forward:
        if far:
            source = at(-half * sign, -dx)
            wait(source)
            send(source, 0, 1 if dx else -1)
        source = at(-(half - 1) * sign, -dx)
        wait(source)
        send(source, 0, 1 if dx else -1)
    for d in range(max(half - 3, 1), half):
        multiply(d)
        multiply(-d)
    multiply(half)

    def part(step):
        to = (narrow + step) % n_narrow
        return pltpu.make_async_remote_copy(
            src_ref=acc.at[pl.ds(pl.multiple_of(to * own_rows, own_rows), own_rows)],
            dst_ref=parts.at[n_narrow - step],
            send_sem=part_sent.at[step],
            recv_sem=part_arrive.at[n_narrow - step],
            device_id={"narrow": to},
            device_id_type=MESH,
        )

    copies = [part(step) for step in range(1, n_narrow)]
    for copy in copies:
        copy.start()
    total = acc[pl.ds(pl.multiple_of(narrow * own_rows, own_rows), own_rows), :]
    for step, copy in zip(range(1, n_narrow), copies):
        pltpu.make_async_remote_copy(
            src_ref=parts.at[step],
            dst_ref=parts.at[step],
            send_sem=part_sent.at[step],
            recv_sem=part_arrive.at[step],
            device_id={"narrow": (narrow + step) % n_narrow},
            device_id_type=MESH,
        ).wait_recv()
        total += parts[step]
    out_ref[...] = jnp.where(keep, total[:, 0:pairs], 0.0)
    for copy in copies:
        copy.wait_send()
    pltpu.make_async_remote_copy(
        src_ref=gathered.at[pl.ds(0, n_wide - 1)],
        dst_ref=gathered.at[pl.ds(0, n_wide - 1)],
        send_sem=sent,
        recv_sem=arrive.at[0],
        device_id={"wide": at(1, 0)},
        device_id_type=MESH,
    ).wait_send()


def shards(n_wide, n_narrow, integrals, amp_tiles, row_orbitals, orb_irrep, occ_pairs, occ_irrep):
    pairs = occ_pairs.shape[0]
    n_rows, n_columns = integrals.shape
    own_rows = n_rows // n_narrow
    operands = (
        integrals, amp_tiles, row_orbitals.T, orb_irrep[None, :], occ_pairs.T, occ_irrep[None, :],
    )
    return pl.pallas_call(
        kernel,
        out_shape=jax.ShapeDtypeStruct((own_rows, pairs), jnp.float32),
        in_specs=[pl.BlockSpec(memory_space=pltpu.HBM)] * len(operands),
        out_specs=pl.BlockSpec(memory_space=pltpu.VMEM),
        scratch_shapes=[
            *(pltpu.VMEM(a.shape, a.dtype) for a in operands[1:]),
            pltpu.VMEM((n_rows, LANES), jnp.int32),
            pltpu.VMEM((LANES // 4, 4 * pairs), jnp.float32),
            pltpu.VMEM((LANES, LANES), jnp.float32),
            pltpu.VMEM((n_wide, pairs, LANES), jnp.bfloat16),
            pltpu.VMEM((n_rows, n_columns), jnp.bfloat16),
            pltpu.VMEM((n_rows, LANES), jnp.float32),
            pltpu.VMEM((n_narrow, own_rows, LANES), jnp.float32),
            pltpu.SemaphoreType.DMA,
            pltpu.SemaphoreType.DMA((len(operands) - 1,)),
            pltpu.SemaphoreType.DMA((n_wide,)),
            pltpu.SemaphoreType.DMA,
            pltpu.SemaphoreType.DMA((n_narrow,)),
            pltpu.SemaphoreType.DMA((n_narrow,)),
        ],
        compiler_params=pltpu.CompilerParams(
            collective_id=0, has_side_effects=True, vmem_limit_bytes=32 << 20
        ),
    )(*operands)


def solution(mesh):
    in_specs = (P("wide", "narrow"), P("narrow", "wide"), P("wide", None), P(), P(), P())
    out_specs = P(("wide", "narrow"), None)
    return jax.shard_map(
        functools.partial(shards, mesh.shape["wide"], mesh.shape["narrow"]),
        mesh=mesh, in_specs=in_specs, out_specs=out_specs, check_vma=False,
    )
```
